512 devices in a mesh: dp: 16 (over x_lo, y), peak: 16 (over z, x_hi), mod: 2 (over core).
Axes of the slice: x: 4 (x_hi: 2, x_lo: 2; x = x_hi * 2 + x_lo), y: 8, z: 8, core: 2. Of those that a mesh axis runs over, the one named last changes fastest.
Arguments:
- hidden_in: bfloat16 [2, 49152, 1024], P('mod', ('dp', 'peak')), parts along dimension 1, may hold values from -31 to 31
- value_bins: int32 [2, 49152], P('mod', ('dp', 'peak')), parts along dimension 1, may hold values from 0 to 50
- mask_flags: int32 [2, 49152], P('mod', ('dp', 'peak')), parts along dimension 1, may hold values 0 or 1
- segment_ids: int32 [2, 256, 192], P('mod', ('dp', 'peak')), parts along dimension 1, may hold values from 0 to 3, never falling along the last dimension, each value on 1 to 96 neighbouring positions
- bin_table: bfloat16 [2, 51, 1024], P('mod'), may hold values from -3 to 3
- mask_vector: bfloat16 [2, 1024], P('mod'), may hold values from -4 to 4
- qkv_weight: bfloat16 [1024, 3072], P('mod'), may hold values from -1 to 1
- out_weight: bfloat16 [1024, 1024], P('mod'), may hold values from -1.5 to 1.5
Outputs:
- update: bfloat16 [2, 49152, 1024], P('mod', ('dp', 'peak')), parts along dimension 1
The draws below stay inside these ranges and needn't reach their ends.
There are 16 independent parts, one for each index of `dp`. The reference program is written for one: setup_inputs(seed, part) draws one part's arguments, and reference() takes and returns one part's arrays. A program takes and returns all parts, laid end to end along the dimension named above; an argument that names none is the same for every part. Nothing has to cross between parts.
Inputs may be any that keep to these rules, and one draw needn't show every extreme that they name: `segment_ids`: in each block of 192 tokens the segments 0 to 3 follow in order, each of 1 to 96 tokens, one of exactly 96.
All inputs are finite; a program needn't handle non-finite values. No bound on the sum of `mask_flags` on one device may be relied on, other than what follows from the above.
Results may differ from the reference program's by a relative error of at most 0.01205.
The reference program's roundings to bfloat16 on the way count: a program that leaves them out, or rounds other values in their place, can miss the bound.
Values may be sent and summed in bfloat16 or wider, within the bound.
A program may use at most 128 MiB of HBM per device.

```python
import math
import jax
import jax.numpy as jnp
import numpy as np
from jax import lax

D = 1024
H = 16
HD = 64
NBINS = 51
TOK_DEV = 192
SEG_DEV = 4
SEG_MOST = 96
LENGTH = 3072
MEMORY = 64
N_PEAK = 16


def draw_hidden_in(key, part):
    shape = (2, LENGTH, D)
    base = jax.random.truncated_normal(jax.random.fold_in(key, 11), -5.0, 5.0, shape, jnp.float32)
    result = base
    return result.astype(jnp.bfloat16)


def draw_qkv_weight(key, part):
    normals = jax.random.truncated_normal(jax.random.fold_in(key, 21), -5.0, 5.0, (D, H, 3, HD), jnp.float32)
    factors = jnp.array([math.sqrt(1.5), math.sqrt(1.5), 1.0], jnp.float32) / math.sqrt(D)
    weights = normals * factors[None, None, :, None]
    return weights.reshape(D, 3 * D).astype(jnp.bfloat16)


def plant(drawn, rng, least, largest):
    dims = drawn.shape
    place = [jax.random.randint(jax.random.fold_in(rng, axis), (), 0, dims[axis]) for axis in range(len(dims))]
    drawn = drawn.at[tuple(place)].set(least)
    longest = dims.index(max(dims))
    place[longest] = (place[longest] + 1) % dims[longest]
    return drawn.at[tuple(place)].set(largest)


def level_of(own_key, shape, shards, least, high):
    loudness, own = 1.0, jax.random.fold_in(own_key, 6)
    for axis_at, shards_of in shards:
        heights = jnp.exp(jax.random.uniform(jax.random.fold_in(own, axis_at), (shards_of,), jnp.float32, least / len(shards), high / len(shards)))
        loudness = loudness * jnp.repeat(heights, shape[axis_at] // shards_of).reshape([-1 if axis == axis_at else 1 for axis in range(len(shape))])
    return loudness


def split_up(number_of, total, reach, slope):
    weights = [(1 << 20) // math.isqrt(grade ** slope) + 1 for grade in range(2, number_of + 1)]
    rest, given = total - reach - (number_of - 1), [1] * (number_of - 1)
    while rest > 0:
        free = [i for i in range(number_of - 1) if given[i] < reach]
        pool, left = sum([weights[i] for i in free]), rest
        for i in free:
            addition = min(reach - given[i], max(1, left * weights[i] // pool), rest)
            given[i] = given[i] + addition
            rest = rest - addition
    return np.array([reach] + given)


def ragged(key, amount, total, reach, slope):
    if amount == 2:
        one = jax.random.randint(key, (), max(1, total - reach), min(reach, total - 1) + 1)
        return jnp.stack([one, total - one])
    tallies = jnp.asarray(split_up(amount, total, reach, slope), jnp.int32)
    couples = (amount - 1) // 2
    giver, sink = tallies[1:1 + 2 * couples:2], tallies[2:2 + 2 * couples:2]
    room = jnp.minimum(giver - 1, reach - sink)
    passed = jax.random.randint(jax.random.fold_in(key, 1), (couples,), 0, 1 << 20) % (room + 1)
    tallies = tallies.at[1:1 + 2 * couples:2].set(giver - passed).at[2:2 + 2 * couples:2].set(sink + passed)
    return tallies[jax.random.permutation(jax.random.fold_in(key, 2), amount)]


def bell_draw(own_key, extent, spread, reach, shards=(), held_as=jnp.bfloat16):
    values = spread * jax.random.normal(own_key, extent, jnp.float32)
    if shards:
        values = values * level_of(own_key, extent, shards, -0.22, 0.18)
    return jnp.clip(values, -reach, reach).astype(held_as)


def setup_inputs(seed: int = 0, part: int = 0) -> dict:
    key_of = jax.random.split(jax.random.key(seed), 9)
    own_keys = jax.random.split(jax.random.fold_in(key_of[8], part), 9)
    return {
        "hidden_in": draw_hidden_in(jax.random.fold_in(jax.random.fold_in(key_of[8], part), 71), part),
        "value_bins": plant(jax.random.randint(own_keys[1], (2, LENGTH), 0, NBINS), jax.random.fold_in(own_keys[1], 1), 0, NBINS - 1).astype(jnp.int32),
        "mask_flags": plant((jax.random.randint(own_keys[2], (2, LENGTH), 0, 100) < 15).astype(jnp.int32), jax.random.fold_in(own_keys[2], 1), 0, 1),
        "segment_ids": jax.vmap(lambda own: jnp.searchsorted(jnp.cumsum(ragged(own, SEG_DEV, TOK_DEV, SEG_MOST, 1)), jnp.arange(TOK_DEV), side="right"))(jax.random.split(own_keys[3], 2 * N_PEAK)).reshape((2, N_PEAK, TOK_DEV)).astype(jnp.int32),
        "bin_table": bell_draw(key_of[4], (2, NBINS, D), 0.5, 3.0, ((0, 2),)),
        "mask_vector": bell_draw(key_of[5], (2, D), 1.0, 4.0, ((0, 2),)),
        "qkv_weight": draw_qkv_weight(jax.random.fold_in(key_of[8], 71), part),
        "out_weight": bell_draw(key_of[7], (D, D), (D // 64) ** -0.5, 1.5, ((0, 2),)),
    }


def embed_tokens(hidden_rows, bin_ids, flag_rows, table, masked_row):
    selector = (bin_ids[:, None] == jnp.arange(NBINS, dtype=jnp.int32)[None, :]).astype(jnp.bfloat16)
    bin_rows = jnp.dot(selector, table, preferred_element_type=jnp.float32)
    chosen = jnp.where(flag_rows[:, None] == 1, masked_row[None, :].astype(jnp.float32), hidden_rows.astype(jnp.float32))
    return (chosen + bin_rows).astype(jnp.bfloat16)


def pool_blocks(key_values, segments):
    blocks = key_values.reshape(N_PEAK, TOK_DEV, 2 * D).astype(jnp.float32)
    selector = (segments[:, None, :] == jnp.arange(SEG_DEV, dtype=jnp.int32)[None, :, None]).astype(jnp.float32)
    sums = jnp.einsum("nst,ntc->nsc", selector, blocks)
    counts = jnp.sum(selector, axis=2)
    pooled = lax.optimization_barrier((sums / counts[:, :, None]).astype(jnp.bfloat16))
    bias = lax.optimization_barrier(jnp.log(counts).astype(jnp.bfloat16))
    return pooled.reshape(MEMORY, H, 2, HD), bias.reshape(MEMORY)


def attend(queries, key_values, pooled, bias):
    score_scale = float(HD) ** -0.5
    key_all = jnp.concatenate([key_values[:, :, 0], pooled[:, :, 0]], axis=0).astype(jnp.float32)
    value_all = jnp.concatenate([key_values[:, :, 1], pooled[:, :, 1]], axis=0).astype(jnp.float32)
    score_bias = jnp.concatenate([jnp.zeros((LENGTH,), jnp.float32), bias.astype(jnp.float32)], axis=0)
    block_size = math.gcd(LENGTH, 256)

    def one_block(query_block):
        scores = jnp.einsum("qhd,khd->qhk", query_block.astype(jnp.float32), key_all) * score_scale
        scores = scores + score_bias[None, None, :]
        row_max = jnp.max(scores, axis=2, keepdims=True)
        weights = jnp.exp(scores - row_max)
        denominator = jnp.sum(weights, axis=2)
        rounded = lax.optimization_barrier(weights.astype(jnp.bfloat16)).astype(jnp.float32)
        numerator = jnp.einsum("qhk,khd->qhd", rounded, value_all)
        return (numerator / denominator[:, :, None]).astype(jnp.bfloat16)

    attended = lax.map(one_block, queries.reshape(LENGTH // block_size, block_size, H, HD))
    return attended.reshape(LENGTH, D)


def reference(hidden_in, value_bins, mask_flags, segment_ids, bin_table, mask_vector, qkv_weight, out_weight):
    query_list = []
    kv_list = []
    pooled_list = []
    bias_list = []
    for modality in range(2):
        embedded = embed_tokens(hidden_in[modality], value_bins[modality], mask_flags[modality], bin_table[modality], mask_vector[modality])
        projected = jnp.dot(embedded, qkv_weight, preferred_element_type=jnp.float32)
        projected = lax.optimization_barrier(projected.astype(jnp.bfloat16)).reshape(LENGTH, H, 3, HD)
        query_list.append(projected[:, :, 0])
        key_values = projected[:, :, 1:3]
        kv_list.append(key_values)
        pooled, bias = pool_blocks(key_values.reshape(LENGTH, 2 * D), segment_ids[modality])
        pooled_list.append(pooled)
        bias_list.append(bias)
    updates = []
    for modality in range(2):
        attended = attend(query_list[modality], kv_list[modality], pooled_list[1 - modality], bias_list[1 - modality])
        updates.append(jnp.dot(attended, out_weight, preferred_element_type=jnp.float32).astype(jnp.bfloat16))
    return jnp.stack(updates, axis=0)
```

```python
import functools

import jax
import jax.numpy as jnp
from jax import lax
from jax.experimental import pallas as pl
from jax.experimental.pallas import tpu as pltpu
from jax.sharding import PartitionSpec as P

H = 16
NBINS = 51
TOK = 192
HALF = TOK // 2
WIDTH = 1024
NP = 16
PAIRS = 8
SELF = 8
GROUP = 4
CHUNK = 384
MESH = pl.DeviceIdType.MESH
F32 = jnp.float32
BF16 = jnp.bfloat16


def dot(a, b):
    return jnp.dot(a, b, preferred_element_type=F32)


def dot_t(a, b):
    return lax.dot_general(a, b, (((1,), (1,)), ((), ())), preferred_element_type=F32)


def low_lanes(rows):
    return lax.broadcasted_iota(jnp.int32, (rows, 128), 1) < 64


def kernel(
    hid, bins, flags, seg, tab, mvec, w, wo, out,
    e_scr, tab_scr, w_own, w_oth, wo_scr, kvs, kvr, qs, qr, pls, plx, plr,
    vt, pk_scr, pvt_scr, bias_scr, qz, s_scr, os, att, acc,
    w_sem, wx_ssem, wx_rsem, wo_sem, wox_ssem, wox_rsem,
    kv_ssem, kv_rsem, q_ssem, q_rsem, px_ssem, px_rsem, pl_ssem, pl_rsem, b_ssem, b_rsem,
):
    p = lax.axis_index("peak")
    m = lax.axis_index("mod")
    z = p // 2
    xh = lax.rem(p, 2)
    other = 1 - m

    def target(i, dx):
        return 2 * lax.rem(z + 4 + i, PAIRS) + lax.rem(xh + dx, 2)

    def source(i, dx):
        return 2 * lax.rem(z + 12 - i, PAIRS) + lax.rem(xh + dx, 2)

    def to_peer(src, dst, ssem, rsem, t):
        return pltpu.make_async_remote_copy(
            src, dst, ssem, rsem, device_id={"peak": t}, device_id_type=MESH
        )

    def to_partner(src, dst, ssem, rsem):
        return pltpu.make_async_remote_copy(
            src, dst, ssem, rsem, device_id={"mod": other}, device_id_type=MESH
        )

    def kv_copy(i, dx):
        k = 2 * i + dx
        t = target(i, dx)
        return to_peer(kvs.at[t], kvr.at[k], kv_ssem.at[k], kv_rsem.at[k], t)

    def q_copy(i, dx):
        k = 2 * i + dx
        t = target(i, dx)
        return to_peer(qs.at[t], qr.at[k], q_ssem.at[k], q_rsem.at[k], t)

    def pool_copy(i, dx):
        k = 2 * i + dx
        t = target(i, dx)
        return to_peer(plx.at[t], plr.at[k], pl_ssem.at[k], pl_rsem.at[k], t)

    def back_copy(i, dx):
        k = 2 * i + dx
        return to_peer(os.at[k], att.at[p], b_ssem.at[k], b_rsem.at[k], source(i, dx))

    def pool_swap(i):
        j = lax.rem(z + 4 + i, PAIRS)
        return to_partner(
            pls.at[pl.ds(2 * j, 2)], plx.at[pl.ds(2 * j, 2)], px_ssem.at[i], px_rsem.at[i]
        )

    def columns(i):
        j = lax.rem(z + 4 + i, PAIRS)
        return w.at[:, pl.ds(pl.multiple_of(j * 384, 128), 384)]

    def w_copy(i):
        return pltpu.make_async_copy(columns(i), w_own.at[i], w_sem.at[i])

    def w_swap(i):
        return to_partner(columns(i), w_oth.at[i], wx_ssem.at[i], wx_rsem.at[i])

    own_rows = pl.ds(pl.multiple_of(m * 512, 512), 512)
    oth_rows = pl.ds(pl.multiple_of(other * 512, 512), 512)
    wo_copy = pltpu.make_async_copy(wo, wo_scr.at[own_rows], wo_sem)
    wo_swap = to_partner(wo, wo_scr.at[own_rows], wox_ssem, wox_rsem)

    barrier = pltpu.get_barrier_semaphore()
    for i in range(PAIRS):
        for dx in range(2):
            if 2 * i + dx != SELF:
                pl.semaphore_signal(
                    barrier, inc=1, device_id={"peak": target(i, dx)}, device_id_type=MESH
                )
    pl.semaphore_signal(barrier, inc=1, device_id={"mod": other}, device_id_type=MESH)

    for i in range(PAIRS):
        w_copy(i).start()
    wo_copy.start()

    tab_scr[...] = jnp.zeros_like(tab_scr)
    tab_scr[0:NBINS] = tab[0]
    row = lax.broadcasted_iota(jnp.int32, (128, TOK), 0)
    onehot = jnp.where(row < 64, (row == bins[...]).astype(F32), (flags[...] == 1).astype(F32))
    picked = onehot.T
    rows_of_bin = dot(picked[:, :64].astype(BF16), tab_scr[...])
    masked = picked[:, 64:65] > 0.5
    chosen = jnp.where(masked, mvec[...].astype(F32), hid[0].astype(F32))
    e_scr[...] = (chosen + rows_of_bin).astype(BF16)

    segment = jnp.bitwise_and(lax.broadcasted_iota(jnp.int32, (16, TOK), 0), 3)
    chosen_seg = (segment == seg[0]).astype(F32)
    counts = jnp.sum(chosen_seg, axis=1, keepdims=True)
    log_counts = jnp.broadcast_to(jnp.log(counts), (16, 128))
    sel = chosen_seg.astype(BF16)
    pool_row = lax.broadcasted_iota(jnp.int32, (16, 128), 0) < 4

    pl.semaphore_wait(barrier, 16)
    for i in range(PAIRS):
        w_swap(i).start()
    wo_swap.start()

    lo = low_lanes(TOK)
    lo_half = low_lanes(HALF)

    def project(i, carry):
        j = lax.rem(z + 4 + i, PAIRS)
        w_copy(i).wait()
        w_swap(i).wait_recv()
        pr = dot(e_scr[:, own_rows], w_own[i]) + dot(e_scr[:, oth_rows], w_oth[i])
        t0, t1, t2 = pr[:, 0:128], pr[:, 128:256], pr[:, 256:384]
        r0 = pltpu.roll(t0, 64, 1)
        r1 = pltpu.roll(t1, 64, 1)
        kv0 = jnp.where(lo, r0, r1).astype(BF16)
        kv1 = t2.astype(BF16)
        kvs[2 * j] = kv0
        kvs[2 * j + 1] = kv1
        for dx in range(2):
            @pl.when(2 * i + dx != SELF)
            def _():
                kv_copy(i, dx).start()
        q0 = jnp.where(lo_half, t0[:HALF], r0[HALF:])
        q1 = jnp.where(lo_half, r1[:HALF], t1[HALF:])
        qs[2 * j] = (q0 * 0.125).astype(BF16)
        qs[2 * j + 1] = (q1 * 0.125).astype(BF16)
        pls[2 * j] = jnp.where(pool_row, dot(sel, kv0) / counts, log_counts).astype(BF16)
        pls[2 * j + 1] = jnp.where(pool_row, dot(sel, kv1) / counts, log_counts).astype(BF16)
        pool_swap(i).start()
        return carry

    lax.fori_loop(0, PAIRS, project, 0)
    kvr[SELF] = kvs[p]
    qr[SELF] = qs[p]

    def forward(i, carry):
        pool_swap(i).wait_recv()
        for dx in range(2):
            @pl.when(2 * i + dx != SELF)
            def _():
                pool_copy(i, dx).start()
        return carry

    lax.fori_loop(0, PAIRS, forward, 0)
    plr[SELF] = plx[p]

    def send_q(i, carry):
        for dx in range(2):
            @pl.when(2 * i + dx != SELF)
            def _():
                q_copy(i, dx).start()
        return carry

    lax.fori_loop(0, PAIRS, send_q, 0)

    def take_values(i, carry):
        for dx in range(2):
            @pl.when(2 * i + dx != SELF)
            def _():
                kv_copy(i, dx).wait_recv()
        block = kvr[pl.ds(2 * i, 2)].reshape(2 * TOK, 128).astype(F32).T
        vt[:, pl.ds(pl.multiple_of(i * 384, 128), 384)] = block[64:128].astype(BF16)
        return carry

    lax.fori_loop(0, PAIRS, take_values, 0)

    def take_pooled(i, carry):
        for dx in range(2):
            @pl.when(2 * i + dx != SELF)
            def _():
                pool_copy(i, dx).wait_recv()
        return carry

    lax.fori_loop(0, PAIRS, take_pooled, 0)
    pooled = plr[...].reshape(NP * 16, 128)
    summary = lax.broadcasted_iota(jnp.int32, (64, 256), 0)
    place = (summary // 4) * 16 + jnp.bitwise_and(summary, 3)
    column = lax.broadcasted_iota(jnp.int32, (64, 256), 1)
    pk = dot((column == place).astype(BF16), pooled)
    pk_scr[...] = pk.astype(BF16)
    bias_scr[...] = dot((column == place + 4).astype(BF16), pooled)
    pk_pad = jnp.concatenate([pk, jnp.zeros((64, 128), F32)], axis=0).T
    pvt_scr[...] = pk_pad[64:128].astype(BF16)

    cols = GROUP * TOK
    n_chunks = NP * TOK // CHUNK

    def attend(g, carry):
        for kk in range(GROUP):
            i = g * (GROUP // 2) + kk // 2
            dx = kk % 2

            @pl.when(2 * i + dx != SELF)
            def _():
                q_copy(i, dx).wait_recv()
            a = qr[2 * i + dx].astype(F32)
            top = jnp.where(lo_half, a, 0.0)
            bottom = jnp.where(lo_half, pltpu.roll(a, 64, 1), 0.0)
            qz[kk * TOK:kk * TOK + HALF] = top.astype(BF16)
            qz[kk * TOK + HALF:(kk + 1) * TOK] = bottom.astype(BF16)
        s_pool = dot_t(pk_scr[...], qz[...]) + bias_scr[:, 0:1]
        m8 = jnp.max(s_pool.reshape(8, 8, cols), axis=0)

        def score(c, m8):
            keys = kvr[pl.ds(c * (CHUNK // TOK), CHUNK // TOK)].reshape(CHUNK, 128)
            s = dot_t(keys, qz[...])
            s_scr[pl.ds(pl.multiple_of(c * CHUNK, CHUNK), CHUNK)] = s
            return jnp.maximum(m8, jnp.max(s.reshape(CHUNK // 8, 8, cols), axis=0))

        m8 = lax.fori_loop(0, n_chunks, score, m8)
        top_score = jnp.max(m8, axis=0, keepdims=True)
        w_pool = jnp.exp(s_pool - top_score)
        l8 = jnp.sum(w_pool.reshape(8, 8, cols), axis=0)
        acc_o = dot(pvt_scr[:, 0:64], w_pool.astype(BF16))

        def weigh(c, state):
            l8, acc_o = state
            s = s_scr[pl.ds(pl.multiple_of(c * CHUNK, CHUNK), CHUNK)]
            wt = jnp.exp(s - top_score)
            l8 = l8 + jnp.sum(wt.reshape(CHUNK // 8, 8, cols), axis=0)
            values = vt[:, pl.ds(pl.multiple_of(c * CHUNK, 128), CHUNK)]
            return l8, acc_o + dot(values, wt.astype(BF16))

        l8, acc_o = lax.fori_loop(0, n_chunks, weigh, (l8, acc_o))
        attended = (acc_o / jnp.sum(l8, axis=0, keepdims=True)).T
        for kk in range(GROUP):
            i = g * (GROUP // 2) + kk // 2
            dx = kk % 2
            rows = attended[kk * TOK:(kk + 1) * TOK]
            packed = jnp.concatenate([rows[:HALF], rows[HALF:]], axis=1).astype(BF16)
            os[2 * i + dx] = packed

            @pl.when(2 * i + dx != SELF)
            def _():
                back_copy(i, dx).start()

            @pl.when(2 * i + dx == SELF)
            def _():
                att[p] = packed
        return carry

    lax.fori_loop(0, NP // GROUP, attend, 0)

    wo_copy.wait()
    wo_swap.wait_recv()
    acc[...] = jnp.zeros_like(acc)

    def finish(i, carry):
        j = lax.rem(z + 4 + i, PAIRS)
        for dx in range(2):
            @pl.when(2 * i + dx != SELF)
            def _():
                back_copy(i, dx).wait_recv()
        a = att[2 * j].astype(F32)
        b = att[2 * j + 1].astype(F32)
        top = jnp.where(lo_half, a, pltpu.roll(b, 64, 1))
        bottom = jnp.where(lo_half, pltpu.roll(a, 64, 1), b)
        rows = jnp.concatenate([top, bottom], axis=0).astype(BF16)
        acc[...] += dot(rows, wo_scr[pl.ds(pl.multiple_of(j * 128, 128), 128)])
        return carry

    lax.fori_loop(0, PAIRS, finish, 0)
    out[0] = acc[...].astype(BF16)

    def drain(i, carry):
        for dx in range(2):
            @pl.when(2 * i + dx != SELF)
            def _():
                kv_copy(i, dx).wait_send()
                q_copy(i, dx).wait_send()
                pool_copy(i, dx).wait_send()
                back_copy(i, dx).wait_send()
        pool_swap(i).wait_send()
        w_swap(i).wait_send()
        return carry

    lax.fori_loop(0, PAIRS, drain, 0)
    wo_swap.wait_send()


def shards(hidden_in, value_bins, mask_flags, segment_ids, bin_table, mask_vector, qkv_weight, out_weight):
    vmem = pl.BlockSpec(memory_space=pltpu.VMEM)
    hbm = pl.BlockSpec(memory_space=pl.ANY)
    dma = pltpu.SemaphoreType.DMA
    return pl.pallas_call(
        kernel,
        out_shape=jax.ShapeDtypeStruct((1, TOK, WIDTH), BF16),
        in_specs=[vmem] * 6 + [hbm] * 2,
        out_specs=vmem,
        scratch_shapes=[
            pltpu.VMEM((TOK, WIDTH), BF16),
            pltpu.VMEM((64, WIDTH), BF16),
            pltpu.VMEM((PAIRS, 512, 384), BF16),
            pltpu.VMEM((PAIRS, 512, 384), BF16),
            pltpu.VMEM((WIDTH, WIDTH), BF16),
            pltpu.VMEM((NP, TOK, 128), BF16),
            pltpu.VMEM((NP, TOK, 128), BF16),
            pltpu.VMEM((NP, HALF, 128), BF16),
            pltpu.VMEM((NP, HALF, 128), BF16),
            pltpu.VMEM((NP, 16, 128), BF16),
            pltpu.VMEM((NP, 16, 128), BF16),
            pltpu.VMEM((NP, 16, 128), BF16),
            pltpu.VMEM((64, NP * TOK), BF16),
            pltpu.VMEM((64, 128), BF16),
            pltpu.VMEM((64, 128), BF16),
            pltpu.VMEM((64, 128), F32),
            pltpu.VMEM((GROUP * TOK, 128), BF16),
            pltpu.VMEM((NP * TOK, GROUP * TOK), F32),
            pltpu.VMEM((NP, HALF, 128), BF16),
            pltpu.VMEM((NP, HALF, 128), BF16),
            pltpu.VMEM((TOK, WIDTH), F32),
            dma((PAIRS,)), dma((PAIRS,)), dma((PAIRS,)),
            dma, dma, dma,
            dma((NP,)), dma((NP,)), dma((NP,)), dma((NP,)),
            dma((PAIRS,)), dma((PAIRS,)), dma((NP,)), dma((NP,)), dma((NP,)), dma((NP,)),
        ],
        compiler_params=pltpu.CompilerParams(
            collective_id=0, has_side_effects=True, vmem_limit_bytes=50 << 20
        ),
        cost_estimate=pl.CostEstimate(
            flops=4 * 10**9, bytes_accessed=10 * 2**20, transcendentals=10**7
        ),
    )(hidden_in, value_bins, mask_flags, segment_ids, bin_table, mask_vector, qkv_weight, out_weight)


def solution(mesh):
    placed = (
        P("mod", ("dp", "peak"), None),
        P("mod", ("dp", "peak")),
        P("mod", ("dp", "peak")),
        P("mod", ("dp", "peak"), None),
        P("mod", None, None),
        P("mod", None),
        P("mod", None),
        P("mod", None),
    )
    return jax.shard_map(
        shards,
        mesh=mesh,
        in_specs=placed,
        out_specs=P("mod", ("dp", "peak"), None),
        check_vma=False,
    )
```

```python
import functools

import jax
import jax.numpy as jnp
from jax import lax
from jax.experimental import pallas as pl
from jax.experimental.pallas import tpu as pltpu
from jax.sharding import PartitionSpec as P

H = 16
NBINS = 51
TOK = 192
HALF = TOK // 2
WIDTH = 1024
NP = 16
PAIRS = 8
SELF = 8
GROUP = 4
CHUNK = 3072
MESH = pl.DeviceIdType.MESH
F32 = jnp.float32
BF16 = jnp.bfloat16


def dot(a, b):
    return jnp.dot(a, b, preferred_element_type=F32)


def dot_t(a, b):
    return lax.dot_general(a, b, (((1,), (1,)), ((), ())), preferred_element_type=F32)


def low_lanes(rows):
    return lax.broadcasted_iota(jnp.int32, (rows, 128), 1) < 64


def kernel(
    hid_in, bins_in, flags_in, seg_in, tab_in, mvec_in, w, wo, out,
    hid, bins, flags, seg, tab, mvec, in_sem,
    e_scr, tab_scr, w_own, w_oth, wo_scr, kvs, kvr, qs, qr, pls, plx, plr,
    vt, pk_scr, pvt_scr, bias_scr, qz, s_scr, os, att, acc,
    w_sem, wx_ssem, wx_rsem, wo_sem, wox_ssem, wox_rsem,
    kv_ssem, kv_rsem, q_ssem, q_rsem, px_ssem, px_rsem, pl_ssem, pl_rsem, b_ssem, b_rsem,
):
    p = lax.axis_index("peak")
    m = lax.axis_index("mod")
    z = p // 2
    xh = lax.rem(p, 2)
    other = 1 - m

    def target(i, dx):
        return 2 * lax.rem(z + 4 + i, PAIRS) + lax.rem(xh + dx, 2)

    def source(i, dx):
        return 2 * lax.rem(z + 12 - i, PAIRS) + lax.rem(xh + dx, 2)

    def to_peer(src, dst, ssem, rsem, t):
        return pltpu.make_async_remote_copy(
            src, dst, ssem, rsem, device_id={"peak": t}, device_id_type=MESH
        )

    def to_partner(src, dst, ssem, rsem):
        return pltpu.make_async_remote_copy(
            src, dst, ssem, rsem, device_id={"mod": other}, device_id_type=MESH
        )

    def kv_copy(i, dx):
        k = 2 * i + dx
        t = target(i, dx)
        return to_peer(kvs.at[t], kvr.at[k], kv_ssem.at[k], kv_rsem.at[k], t)

    def q_copy(i, dx):
        k = 2 * i + dx
        t = target(i, dx)
        return to_peer(qs.at[t], qr.at[k], q_ssem.at[k], q_rsem.at[k], t)

    def pool_copy(i, dx):
        k = 2 * i + dx
        t = target(i, dx)
        return to_peer(plx.at[t], plr.at[k], pl_ssem.at[k], pl_rsem.at[k], t)

    def back_copy(i, dx):
        k = 2 * i + dx
        return to_peer(os.at[k], att.at[p], b_ssem.at[k], b_rsem.at[k], source(i, dx))

    def pool_swap(i):
        j = lax.rem(z + 4 + i, PAIRS)
        return to_partner(
            pls.at[pl.ds(2 * j, 2)], plx.at[pl.ds(2 * j, 2)], px_ssem.at[i], px_rsem.at[i]
        )

    def columns(i):
        j = lax.rem(z + 4 + i, PAIRS)
        return w.at[:, pl.ds(pl.multiple_of(j * 384, 128), 384)]

    def w_copy(i):
        return pltpu.make_async_copy(columns(i), w_own.at[i], w_sem.at[i])

    def w_swap(i):
        return to_partner(columns(i), w_oth.at[i], wx_ssem.at[i], wx_rsem.at[i])

    own_rows = pl.ds(pl.multiple_of(m * 512, 512), 512)
    oth_rows = pl.ds(pl.multiple_of(other * 512, 512), 512)
    wo_copy = pltpu.make_async_copy(wo, wo_scr.at[own_rows], wo_sem)
    wo_swap = to_partner(wo, wo_scr.at[own_rows], wox_ssem, wox_rsem)

    barrier = pltpu.get_barrier_semaphore()
    for i in range(PAIRS):
        for dx in range(2):
            if 2 * i + dx != SELF:
                pl.semaphore_signal(
                    barrier, inc=1, device_id={"peak": target(i, dx)}, device_id_type=MESH
                )
    pl.semaphore_signal(barrier, inc=1, device_id={"mod": other}, device_id_type=MESH)

    loads = [
        pltpu.make_async_copy(source_ref, place, in_sem.at[n])
        for n, (source_ref, place) in enumerate((
            (bins_in, bins), (flags_in, flags), (tab_in, tab), (seg_in, seg), (mvec_in, mvec), (hid_in, hid)
        ))
    ]
    for load in loads:
        load.start()
    for i in range(PAIRS):
        w_copy(i).start()
    wo_copy.start()
    for load in loads:
        load.wait()

    tab_scr[...] = jnp.zeros_like(tab_scr)
    tab_scr[0:NBINS] = tab[0]
    row = lax.broadcasted_iota(jnp.int32, (128, TOK), 0)
    onehot = jnp.where(row < 64, (row == bins[...]).astype(F32), (flags[...] == 1).astype(F32))
    picked = onehot.T
    rows_of_bin = dot(picked[:, :64].astype(BF16), tab_scr[...])
    masked = picked[:, 64:65] > 0.5
    chosen = jnp.where(masked, mvec[...].astype(F32), hid[0].astype(F32))
    e_scr[...] = (chosen + rows_of_bin).astype(BF16)

    segment = jnp.bitwise_and(lax.broadcasted_iota(jnp.int32, (16, TOK), 0), 3)
    chosen_seg = (segment == seg[0]).astype(F32)
    counts = jnp.sum(chosen_seg, axis=1, keepdims=True)
    log_counts = jnp.broadcast_to(jnp.log(counts), (16, 128))
    sel = chosen_seg.astype(BF16)
    pool_row = lax.broadcasted_iota(jnp.int32, (16, 128), 0) < 4

    pl.semaphore_wait(barrier, 16)
    for i in range(PAIRS):
        w_swap(i).start()
    wo_swap.start()

    lo = low_lanes(TOK)
    lo_half = low_lanes(HALF)

    def project(i, carry):
        j = lax.rem(z + 4 + i, PAIRS)
        w_copy(i).wait()
        w_swap(i).wait_recv()
        pr = dot(e_scr[:, own_rows], w_own[i]) + dot(e_scr[:, oth_rows], w_oth[i])
        t0, t1, t2 = pr[:, 0:128], pr[:, 128:256], pr[:, 256:384]
        r0 = pltpu.roll(t0, 64, 1)
        r1 = pltpu.roll(t1, 64, 1)
        kv0 = jnp.where(lo, r0, r1).astype(BF16)
        kv1 = t2.astype(BF16)
        kvs[2 * j] = kv0
        kvs[2 * j + 1] = kv1
        for dx in range(2):
            @pl.when(2 * i + dx != SELF)
            def _():
                kv_copy(i, dx).start()
        q0 = jnp.where(lo_half, t0[:HALF], r0[HALF:])
        q1 = jnp.where(lo_half, r1[:HALF], t1[HALF:])
        qs[2 * j] = (q0 * 0.125).astype(BF16)
        qs[2 * j + 1] = (q1 * 0.125).astype(BF16)
        pls[2 * j] = jnp.where(pool_row, dot(sel, kv0) / counts, log_counts).astype(BF16)
        pls[2 * j + 1] = jnp.where(pool_row, dot(sel, kv1) / counts, log_counts).astype(BF16)
        pool_swap(i).start()
        return carry

    lax.fori_loop(0, PAIRS, project, 0)
    kvr[SELF] = kvs[p]
    qr[SELF] = qs[p]

    def forward(i, carry):
        pool_swap(i).wait_recv()
        for dx in range(2):
            @pl.when(2 * i + dx != SELF)
            def _():
                pool_copy(i, dx).start()
        return carry

    lax.fori_loop(0, PAIRS, forward, 0)
    plr[SELF] = plx[p]

    def send_q(i, carry):
        for dx in range(2):
            @pl.when(2 * i + dx != SELF)
            def _():
                q_copy(i, dx).start()
        return carry

    lax.fori_loop(0, PAIRS, send_q, 0)

    def take_values(i, carry):
        for dx in range(2):
            @pl.when(2 * i + dx != SELF)
            def _():
                kv_copy(i, dx).wait_recv()
        block = kvr[pl.ds(2 * i, 2)].reshape(2 * TOK, 128).astype(F32).T
        vt[:, pl.ds(pl.multiple_of(i * 384, 128), 384)] = block[64:128].astype(BF16)
        return carry

    lax.fori_loop(0, PAIRS, take_values, 0)

    def take_pooled(i, carry):
        for dx in range(2):
            @pl.when(2 * i + dx != SELF)
            def _():
                pool_copy(i, dx).wait_recv()
        return carry

    lax.fori_loop(0, PAIRS, take_pooled, 0)
    pooled = plr[...].reshape(NP * 16, 128)
    summary = lax.broadcasted_iota(jnp.int32, (64, 256), 0)
    place = (summary // 4) * 16 + jnp.bitwise_and(summary, 3)
    column = lax.broadcasted_iota(jnp.int32, (64, 256), 1)
    pk = dot((column == place).astype(BF16), pooled)
    pk_scr[...] = pk.astype(BF16)
    bias_scr[...] = dot((column == place + 4).astype(BF16), pooled)
    pk_pad = jnp.concatenate([pk, jnp.zeros((64, 128), F32)], axis=0).T
    pvt_scr[...] = pk_pad[64:128].astype(BF16)

    cols = GROUP * TOK
    n_chunks = NP * TOK // CHUNK

    def attend(g, carry):
        for kk in range(GROUP):
            i = g * (GROUP // 2) + kk // 2
            dx = kk % 2

            @pl.when(2 * i + dx != SELF)
            def _():
                q_copy(i, dx).wait_recv()
            a = qr[2 * i + dx].astype(F32)
            top = jnp.where(lo_half, a, 0.0)
            bottom = jnp.where(lo_half, pltpu.roll(a, 64, 1), 0.0)
            qz[kk * TOK:kk * TOK + HALF] = top.astype(BF16)
            qz[kk * TOK + HALF:(kk + 1) * TOK] = bottom.astype(BF16)
        s_pool = dot_t(pk_scr[...], qz[...]) + bias_scr[:, 0:1]
        m8 = jnp.max(s_pool.reshape(8, 8, cols), axis=0)

        def score(c, m8):
            keys = kvr[pl.ds(c * (CHUNK // TOK), CHUNK // TOK)].reshape(CHUNK, 128)
            s = dot_t(keys, qz[...])
            s_scr[pl.ds(pl.multiple_of(c * CHUNK, CHUNK), CHUNK)] = s
            return jnp.maximum(m8, jnp.max(s.reshape(CHUNK // 8, 8, cols), axis=0))

        m8 = lax.fori_loop(0, n_chunks, score, m8)
        top_score = jnp.max(m8, axis=0, keepdims=True)
        w_pool = jnp.exp(s_pool - top_score)
        l8 = jnp.sum(w_pool.reshape(8, 8, cols), axis=0)
        acc_o = dot(pvt_scr[:, 0:64], w_pool.astype(BF16))

        def weigh(c, state):
            l8, acc_o = state
            s = s_scr[pl.ds(pl.multiple_of(c * CHUNK, CHUNK), CHUNK)]
            wt = jnp.exp(s - top_score)
            l8 = l8 + jnp.sum(wt.reshape(CHUNK // 8, 8, cols), axis=0)
            values = vt[:, pl.ds(pl.multiple_of(c * CHUNK, 128), CHUNK)]
            return l8, acc_o + dot(values, wt.astype(BF16))

        l8, acc_o = lax.fori_loop(0, n_chunks, weigh, (l8, acc_o))
        attended = (acc_o / jnp.sum(l8, axis=0, keepdims=True)).T
        for kk in range(GROUP):
            i = g * (GROUP // 2) + kk // 2
            dx = kk % 2
            rows = attended[kk * TOK:(kk + 1) * TOK]
            packed = jnp.concatenate([rows[:HALF], rows[HALF:]], axis=1).astype(BF16)
            os[2 * i + dx] = packed

            @pl.when(2 * i + dx != SELF)
            def _():
                back_copy(i, dx).start()

            @pl.when(2 * i + dx == SELF)
            def _():
                att[p] = packed
        return carry

    lax.fori_loop(0, NP // GROUP, attend, 0)

    wo_copy.wait()
    wo_swap.wait_recv()
    acc[...] = jnp.zeros_like(acc)

    def finish(i, carry):
        j = lax.rem(z + 4 + i, PAIRS)
        for dx in range(2):
            @pl.when(2 * i + dx != SELF)
            def _():
                back_copy(i, dx).wait_recv()
        a = att[2 * j].astype(F32)
        b = att[2 * j + 1].astype(F32)
        top = jnp.where(lo_half, a, pltpu.roll(b, 64, 1))
        bottom = jnp.where(lo_half, pltpu.roll(a, 64, 1), b)
        rows = jnp.concatenate([top, bottom], axis=0).astype(BF16)
        acc[...] += dot(rows, wo_scr[pl.ds(pl.multiple_of(j * 128, 128), 128)])
        return carry

    lax.fori_loop(0, PAIRS, finish, 0)
    out[0] = acc[...].astype(BF16)

    def drain(i, carry):
        for dx in range(2):
            @pl.when(2 * i + dx != SELF)
            def _():
                kv_copy(i, dx).wait_send()
                q_copy(i, dx).wait_send()
                pool_copy(i, dx).wait_send()
                back_copy(i, dx).wait_send()
        pool_swap(i).wait_send()
        w_swap(i).wait_send()
        return carry

    lax.fori_loop(0, PAIRS, drain, 0)
    wo_swap.wait_send()


def shards(hidden_in, value_bins, mask_flags, segment_ids, bin_table, mask_vector, qkv_weight, out_weight):
    vmem = pl.BlockSpec(memory_space=pltpu.VMEM)
    hbm = pl.BlockSpec(memory_space=pltpu.MemorySpace.HBM)
    dma = pltpu.SemaphoreType.DMA
    return pl.pallas_call(
        kernel,
        out_shape=jax.ShapeDtypeStruct((1, TOK, WIDTH), BF16),
        in_specs=[hbm] * 8,
        out_specs=vmem,
        scratch_shapes=[
            pltpu.VMEM(hidden_in.shape, BF16),
            pltpu.VMEM(value_bins.shape, jnp.int32),
            pltpu.VMEM(mask_flags.shape, jnp.int32),
            pltpu.VMEM(segment_ids.shape, jnp.int32),
            pltpu.VMEM(bin_table.shape, BF16),
            pltpu.VMEM(mask_vector.shape, BF16),
            dma((6,)),
            pltpu.VMEM((TOK, WIDTH), BF16),
            pltpu.VMEM((64, WIDTH), BF16),
            pltpu.VMEM((PAIRS, 512, 384), BF16),
            pltpu.VMEM((PAIRS, 512, 384), BF16),
            pltpu.VMEM((WIDTH, WIDTH), BF16),
            pltpu.VMEM((NP, TOK, 128), BF16),
            pltpu.VMEM((NP, TOK, 128), BF16),
            pltpu.VMEM((NP, HALF, 128), BF16),
            pltpu.VMEM((NP, HALF, 128), BF16),
            pltpu.VMEM((NP, 16, 128), BF16),
            pltpu.VMEM((NP, 16, 128), BF16),
            pltpu.VMEM((NP, 16, 128), BF16),
            pltpu.VMEM((64, NP * TOK), BF16),
            pltpu.VMEM((64, 128), BF16),
            pltpu.VMEM((64, 128), BF16),
            pltpu.VMEM((64, 128), F32),
            pltpu.VMEM((GROUP * TOK, 128), BF16),
            pltpu.VMEM((NP * TOK, GROUP * TOK), F32),
            pltpu.VMEM((NP, HALF, 128), BF16),
            pltpu.VMEM((NP, HALF, 128), BF16),
            pltpu.VMEM((TOK, WIDTH), F32),
            dma((PAIRS,)), dma((PAIRS,)), dma((PAIRS,)),
            dma, dma, dma,
            dma((NP,)), dma((NP,)), dma((NP,)), dma((NP,)),
            dma((PAIRS,)), dma((PAIRS,)), dma((NP,)), dma((NP,)), dma((NP,)), dma((NP,)),
        ],
        compiler_params=pltpu.CompilerParams(
            collective_id=0, has_side_effects=True, vmem_limit_bytes=64 << 20
        ),
        cost_estimate=pl.CostEstimate(
            flops=4 * 10**9, bytes_accessed=10 * 2**20, transcendentals=10**7
        ),
    )(hidden_in, value_bins, mask_flags, segment_ids, bin_table, mask_vector, qkv_weight, out_weight)


def solution(mesh):
    placed = (
        P("mod", ("dp", "peak"), None),
        P("mod", ("dp", "peak")),
        P("mod", ("dp", "peak")),
        P("mod", ("dp", "peak"), None),
        P("mod", None, None),
        P("mod", None),
        P("mod", None),
        P("mod", None),
    )
    return jax.shard_map(
        shards,
        mesh=mesh,
        in_specs=placed,
        out_specs=P("mod", ("dp", "peak"), None),
        check_vma=False,
    )
```

```python
import functools

import jax
import jax.numpy as jnp
from jax import lax
from jax.experimental import pallas as pl
from jax.experimental.pallas import tpu as pltpu
from jax.sharding import PartitionSpec as P

H = 16
NBINS = 51
TOK = 192
HALF = TOK // 2
WIDTH = 1024
NP = 16
PAIRS = 8
SELF = 2
GROUP = 4
CHUNK = 3072
MESH = pl.DeviceIdType.MESH
F32 = jnp.float32
BF16 = jnp.bfloat16


def dot(a, b):
    return jnp.dot(a, b, preferred_element_type=F32)


def dot_t(a, b):
    return lax.dot_general(a, b, (((1,), (1,)), ((), ())), preferred_element_type=F32)


def low_lanes(rows):
    return lax.broadcasted_iota(jnp.int32, (rows, 128), 1) < 64


def kernel(
    hid_in, bins_in, flags_in, seg_in, tab_in, mvec_in, w, wo, out,
    hid, bins, flags, seg, tab, mvec, in_sem,
    e_scr, tab_scr, w_own, w_oth, wo_scr, kvs, kvr, qs, qr, pls, plx, plr,
    vt, pk_scr, pvt_scr, bias_scr, qz, s_scr, os, att,
    w_sem, wx_ssem, wx_rsem, wo_sem, wox_ssem, wox_rsem,
    kv_ssem, kv_rsem, q_ssem, q_rsem, px_ssem, px_rsem, pl_ssem, pl_rsem, b_ssem, b_rsem,
):
    p = lax.axis_index("peak")
    m = lax.axis_index("mod")
    z = p // 2
    xh = lax.rem(p, 2)
    other = 1 - m

    def step(i):
        near, odd = i // 2, i % 2
        return 4 + (2 * odd - 1) * near + 4 * odd * ((3 - near) // 3)

    def pair_at(i):
        return lax.rem(z + step(i), PAIRS)

    def target(i, dx):
        return 2 * pair_at(i) + lax.rem(xh + dx, 2)

    def source(i, dx):
        return 2 * lax.rem(z + 16 - step(i), PAIRS) + lax.rem(xh + dx, 2)

    def to_peer(src, dst, ssem, rsem, t):
        return pltpu.make_async_remote_copy(
            src, dst, ssem, rsem, device_id={"peak": t}, device_id_type=MESH
        )

    def to_partner(src, dst, ssem, rsem):
        return pltpu.make_async_remote_copy(
            src, dst, ssem, rsem, device_id={"mod": other}, device_id_type=MESH
        )

    def kv_copy(i, dx):
        k = 2 * i + dx
        t = target(i, dx)
        return to_peer(kvs.at[t], kvr.at[k], kv_ssem.at[k], kv_rsem.at[k], t)

    def q_copy(i, dx):
        k = 2 * i + dx
        t = target(i, dx)
        return to_peer(qs.at[t], qr.at[k], q_ssem.at[k], q_rsem.at[k], t)

    def pool_copy(i, dx):
        k = 2 * i + dx
        t = target(i, dx)
        return to_peer(plx.at[t], plr.at[k], pl_ssem.at[k], pl_rsem.at[k], t)

    def back_copy(i, dx):
        k = 2 * i + dx
        return to_peer(os.at[k], att.at[p], b_ssem.at[k], b_rsem.at[k], source(i, dx))

    def pool_swap(i):
        j = pair_at(i)
        return to_partner(
            pls.at[pl.ds(2 * j, 2)], plx.at[pl.ds(2 * j, 2)], px_ssem.at[i], px_rsem.at[i]
        )

    def columns(i):
        j = pair_at(i)
        return w.at[:, pl.ds(pl.multiple_of(j * 384, 128), 384)]

    def w_copy(i):
        return pltpu.make_async_copy(columns(i), w_own.at[i], w_sem.at[i])

    def w_swap(i):
        return to_partner(columns(i), w_oth.at[i], wx_ssem.at[i], wx_rsem.at[i])

    own_rows = pl.ds(pl.multiple_of(m * 512, 512), 512)
    oth_rows = pl.ds(pl.multiple_of(other * 512, 512), 512)
    wo_copy = pltpu.make_async_copy(wo, wo_scr.at[own_rows], wo_sem)
    wo_swap = to_partner(wo, wo_scr.at[own_rows], wox_ssem, wox_rsem)

    barrier = pltpu.get_barrier_semaphore()
    for i in range(PAIRS):
        for dx in range(2):
            if 2 * i + dx != SELF:
                pl.semaphore_signal(
                    barrier, inc=1, device_id={"peak": target(i, dx)}, device_id_type=MESH
                )
    pl.semaphore_signal(barrier, inc=1, device_id={"mod": other}, device_id_type=MESH)

    loads = [
        pltpu.make_async_copy(source_ref, place, in_sem.at[n])
        for n, (source_ref, place) in enumerate((
            (bins_in, bins), (flags_in, flags), (tab_in, tab), (seg_in, seg), (mvec_in, mvec), (hid_in, hid)
        ))
    ]
    for load in loads:
        load.start()
    for i in range(PAIRS):
        w_copy(i).start()
    wo_copy.start()
    for load in loads:
        load.wait()

    tab_scr[...] = jnp.zeros_like(tab_scr)
    tab_scr[0:NBINS] = tab[0]
    row = lax.broadcasted_iota(jnp.int32, (128, TOK), 0)
    onehot = jnp.where(row < 64, (row == bins[...]).astype(F32), (flags[...] == 1).astype(F32))
    picked = onehot.T
    rows_of_bin = dot(picked[:, :64].astype(BF16), tab_scr[...])
    masked = picked[:, 64:65] > 0.5
    chosen = jnp.where(masked, mvec[...].astype(F32), hid[0].astype(F32))
    e_scr[...] = (chosen + rows_of_bin).astype(BF16)

    segment = jnp.bitwise_and(lax.broadcasted_iota(jnp.int32, (16, TOK), 0), 3)
    chosen_seg = (segment == seg[0]).astype(F32)
    counts = jnp.sum(chosen_seg, axis=1, keepdims=True)
    log_counts = jnp.broadcast_to(jnp.log(counts), (16, 128))
    sel = chosen_seg.astype(BF16)
    pool_row = lax.broadcasted_iota(jnp.int32, (16, 128), 0) < 4

    pl.semaphore_wait(barrier, 16)
    for i in range(PAIRS):
        w_swap(i).start()
    wo_swap.start()

    lo = low_lanes(TOK)
    lo_half = low_lanes(HALF)

    def project(i, carry):
        j = pair_at(i)
        w_copy(i).wait()
        w_swap(i).wait_recv()
        pr = dot(e_scr[:, own_rows], w_own[i]) + dot(e_scr[:, oth_rows], w_oth[i])
        t0, t1, t2 = pr[:, 0:128], pr[:, 128:256], pr[:, 256:384]
        r0 = pltpu.roll(t0, 64, 1)
        r1 = pltpu.roll(t1, 64, 1)
        kv0 = jnp.where(lo, r0, r1).astype(BF16)
        kv1 = t2.astype(BF16)
        kvs[2 * j] = kv0
        kvs[2 * j + 1] = kv1
        for dx in range(2):
            @pl.when(2 * i + dx != SELF)
            def _():
                kv_copy(i, dx).start()
        q0 = jnp.where(lo_half, t0[:HALF], r0[HALF:])
        q1 = jnp.where(lo_half, r1[:HALF], t1[HALF:])
        qs[2 * j] = (q0 * 0.125).astype(BF16)
        qs[2 * j + 1] = (q1 * 0.125).astype(BF16)
        pls[2 * j] = jnp.where(pool_row, dot(sel, kv0) / counts, log_counts).astype(BF16)
        pls[2 * j + 1] = jnp.where(pool_row, dot(sel, kv1) / counts, log_counts).astype(BF16)
        pool_swap(i).start()
        return carry

    lax.fori_loop(0, PAIRS, project, 0)
    kvr[SELF] = kvs[p]
    qr[SELF] = qs[p]

    def forward(i, carry):
        pool_swap(i).wait_recv()
        for dx in range(2):
            @pl.when(2 * i + dx != SELF)
            def _():
                pool_copy(i, dx).start()
        return carry

    lax.fori_loop(0, PAIRS, forward, 0)
    plr[SELF] = plx[p]

    def sent_kv(i, carry):
        for dx in range(2):
            @pl.when(2 * i + dx != SELF)
            def _():
                kv_copy(i, dx).wait_send()
        return carry

    lax.fori_loop(0, PAIRS, sent_kv, 0)

    def each_in(g, action):
        for kk in range(GROUP):
            i = g * (GROUP // 2) + kk // 2
            dx = kk % 2

            @pl.when(2 * i + dx != SELF)
            def _():
                action(i, dx)

    each_in(0, lambda i, dx: q_copy(i, dx).start())
    each_in(1, lambda i, dx: q_copy(i, dx).start())

    def take_values(i, carry):
        for dx in range(2):
            @pl.when(2 * i + dx != SELF)
            def _():
                kv_copy(i, dx).wait_recv()
        block = kvr[pl.ds(2 * i, 2)].reshape(2 * TOK, 128).astype(F32).T
        vt[:, pl.ds(pl.multiple_of(i * 384, 128), 384)] = block[64:128].astype(BF16)
        return carry

    lax.fori_loop(0, PAIRS, take_values, 0)

    def take_pooled(i, carry):
        for dx in range(2):
            @pl.when(2 * i + dx != SELF)
            def _():
                pool_copy(i, dx).wait_recv()
        return carry

    lax.fori_loop(0, PAIRS, take_pooled, 0)
    pooled = plr[...].reshape(NP * 16, 128)
    summary = lax.broadcasted_iota(jnp.int32, (64, 256), 0)
    place = (summary // 4) * 16 + jnp.bitwise_and(summary, 3)
    column = lax.broadcasted_iota(jnp.int32, (64, 256), 1)
    pk = dot((column == place).astype(BF16), pooled)
    pk_scr[...] = pk.astype(BF16)
    bias_scr[...] = dot((column == place + 4).astype(BF16), pooled)
    pk_pad = jnp.concatenate([pk, jnp.zeros((64, 128), F32)], axis=0).T
    pvt_scr[...] = pk_pad[64:128].astype(BF16)

    cols = GROUP * TOK
    n_chunks = NP * TOK // CHUNK

    def attend(g, carry):
        each_in(g, lambda i, dx: q_copy(i, dx).wait_recv())

        @pl.when(g == 0)
        def _():
            each_in(2, lambda i, dx: q_copy(i, dx).start())
            each_in(3, lambda i, dx: q_copy(i, dx).start())
        for kk in range(GROUP):
            i = g * (GROUP // 2) + kk // 2
            dx = kk % 2

            a = qr[2 * i + dx].astype(F32)
            top = jnp.where(lo_half, a, 0.0)
            bottom = jnp.where(lo_half, pltpu.roll(a, 64, 1), 0.0)
            qz[kk * TOK:kk * TOK + HALF] = top.astype(BF16)
            qz[kk * TOK + HALF:(kk + 1) * TOK] = bottom.astype(BF16)
        s_pool = dot_t(pk_scr[...], qz[...]) + bias_scr[:, 0:1]
        m8 = jnp.max(s_pool.reshape(8, 8, cols), axis=0)

        def score(c, m8):
            keys = kvr[pl.ds(c * (CHUNK // TOK), CHUNK // TOK)].reshape(CHUNK, 128)
            s = dot_t(keys, qz[...])
            s_scr[pl.ds(pl.multiple_of(c * CHUNK, CHUNK), CHUNK)] = s
            return jnp.maximum(m8, jnp.max(s.reshape(CHUNK // 8, 8, cols), axis=0))

        m8 = lax.fori_loop(0, n_chunks, score, m8)
        top_score = jnp.max(m8, axis=0, keepdims=True)
        w_pool = jnp.exp(s_pool - top_score)
        l8 = jnp.sum(w_pool.reshape(8, 8, cols), axis=0)
        acc_o = dot(pvt_scr[:, 0:64], w_pool.astype(BF16))

        def weigh(c, state):
            l8, acc_o = state
            s = s_scr[pl.ds(pl.multiple_of(c * CHUNK, CHUNK), CHUNK)]
            wt = jnp.exp(s - top_score)
            l8 = l8 + jnp.sum(wt.reshape(CHUNK // 8, 8, cols), axis=0)
            values = vt[:, pl.ds(pl.multiple_of(c * CHUNK, 128), CHUNK)]
            return l8, acc_o + dot(values, wt.astype(BF16))

        l8, acc_o = lax.fori_loop(0, n_chunks, weigh, (l8, acc_o))
        attended = (acc_o / jnp.sum(l8, axis=0, keepdims=True)).T
        for kk in range(GROUP):
            i = g * (GROUP // 2) + kk // 2
            dx = kk % 2
            rows = attended[kk * TOK:(kk + 1) * TOK]
            packed = jnp.concatenate([rows[:HALF], rows[HALF:]], axis=1).astype(BF16)
            os[2 * i + dx] = packed

            @pl.when(2 * i + dx != SELF)
            def _():
                back_copy(i, dx).start()

            @pl.when(2 * i + dx == SELF)
            def _():
                att[p] = packed
        return carry

    lax.fori_loop(0, NP // GROUP, attend, 0)


    def finish(i, carry):
        j = pair_at(i)
        for dx in range(2):
            @pl.when(2 * i + dx != SELF)
            def _():
                back_copy(i, dx).wait_recv()
        a = att[2 * j].astype(F32)
        b = att[2 * j + 1].astype(F32)
        top = jnp.where(lo_half, a, pltpu.roll(b, 64, 1))
        bottom = jnp.where(lo_half, pltpu.roll(a, 64, 1), b)
        rows = jnp.concatenate([top, bottom], axis=0).astype(BF16)
        e_scr[:, pl.ds(pl.multiple_of(j * 128, 128), 128)] = rows
        return carry

    lax.fori_loop(0, PAIRS, finish, 0)
    wo_copy.wait()
    wo_swap.wait_recv()
    out[0] = dot(e_scr[...], wo_scr[...]).astype(BF16)

    def drain(i, carry):
        for dx in range(2):
            @pl.when(2 * i + dx != SELF)
            def _():
                q_copy(i, dx).wait_send()
                pool_copy(i, dx).wait_send()
                back_copy(i, dx).wait_send()
        pool_swap(i).wait_send()
        w_swap(i).wait_send()
        return carry

    lax.fori_loop(0, PAIRS, drain, 0)
    wo_swap.wait_send()


def shards(hidden_in, value_bins, mask_flags, segment_ids, bin_table, mask_vector, qkv_weight, out_weight):
    vmem = pl.BlockSpec(memory_space=pltpu.VMEM)
    hbm = pl.BlockSpec(memory_space=pltpu.MemorySpace.HBM)
    dma = pltpu.SemaphoreType.DMA
    return pl.pallas_call(
        kernel,
        out_shape=jax.ShapeDtypeStruct((1, TOK, WIDTH), BF16),
        in_specs=[hbm] * 8,
        out_specs=vmem,
        scratch_shapes=[
            pltpu.VMEM(hidden_in.shape, BF16),
            pltpu.VMEM(value_bins.shape, jnp.int32),
            pltpu.VMEM(mask_flags.shape, jnp.int32),
            pltpu.VMEM(segment_ids.shape, jnp.int32),
            pltpu.VMEM(bin_table.shape, BF16),
            pltpu.VMEM(mask_vector.shape, BF16),
            dma((6,)),
            pltpu.VMEM((TOK, WIDTH), BF16),
            pltpu.VMEM((64, WIDTH), BF16),
            pltpu.VMEM((PAIRS, 512, 384), BF16),
            pltpu.VMEM((PAIRS, 512, 384), BF16),
            pltpu.VMEM((WIDTH, WIDTH), BF16),
            pltpu.VMEM((NP, TOK, 128), BF16),
            pltpu.VMEM((NP, TOK, 128), BF16),
            pltpu.VMEM((NP, HALF, 128), BF16),
            pltpu.VMEM((NP, HALF, 128), BF16),
            pltpu.VMEM((NP, 16, 128), BF16),
            pltpu.VMEM((NP, 16, 128), BF16),
            pltpu.VMEM((NP, 16, 128), BF16),
            pltpu.VMEM((64, NP * TOK), BF16),
            pltpu.VMEM((64, 128), BF16),
            pltpu.VMEM((64, 128), BF16),
            pltpu.VMEM((64, 128), F32),
            pltpu.VMEM((GROUP * TOK, 128), BF16),
            pltpu.VMEM((NP * TOK, GROUP * TOK), F32),
            pltpu.VMEM((NP, HALF, 128), BF16),
            pltpu.VMEM((NP, HALF, 128), BF16),
            dma((PAIRS,)), dma((PAIRS,)), dma((PAIRS,)),
            dma, dma, dma,
            dma((NP,)), dma((NP,)), dma((NP,)), dma((NP,)),
            dma((PAIRS,)), dma((PAIRS,)), dma((NP,)), dma((NP,)), dma((NP,)), dma((NP,)),
        ],
        compiler_params=pltpu.CompilerParams(
            collective_id=0, has_side_effects=True, vmem_limit_bytes=48 << 20
        ),
        cost_estimate=pl.CostEstimate(
            flops=4 * 10**9, bytes_accessed=10 * 2**20, transcendentals=10**7
        ),
    )(*[
        pltpu.with_memory_space_constraint(x, pltpu.MemorySpace.HBM)
        for x in (
            hidden_in, value_bins, mask_flags, segment_ids,
            bin_table, mask_vector, qkv_weight, out_weight,
        )
    ])


def solution(mesh):
    placed = (
        P("mod", ("dp", "peak"), None),
        P("mod", ("dp", "peak")),
        P("mod", ("dp", "peak")),
        P("mod", ("dp", "peak"), None),
        P("mod", None, None),
        P("mod", None),
        P("mod", None),
        P("mod", None),
    )
    return jax.shard_map(
        shards,
        mesh=mesh,
        in_specs=placed,
        out_specs=P("mod", ("dp", "peak"), None),
        check_vma=False,
    )
```

```python
import functools

import jax
import jax.numpy as jnp
from jax import lax
from jax.experimental import pallas as pl
from jax.experimental.pallas import tpu as pltpu
from jax.sharding import PartitionSpec as P

H = 16
NBINS = 51
TOK = 192
HALF = TOK // 2
WIDTH = 1024
NP = 16
PAIRS = 8
SELF = 2
GROUP = 4
CHUNK = 3072
MESH = pl.DeviceIdType.MESH
F32 = jnp.float32
BF16 = jnp.bfloat16


def dot(a, b):
    return jnp.dot(a, b, preferred_element_type=F32)


def dot_t(a, b):
    return lax.dot_general(a, b, (((1,), (1,)), ((), ())), preferred_element_type=F32)


def low_lanes(rows):
    return lax.broadcasted_iota(jnp.int32, (rows, 128), 1) < 64


def kernel(
    hid_in, bins_in, flags_in, seg_in, tab_in, mvec_in, w, wo, out,
    hid, bins, flags, seg, tab, mvec, in_sem,
    e_scr, tab_scr, w_own, w_oth, wo_scr, kvs, kvr, qs, qr, pls, plx, plr,
    vt, pk_scr, pvt_scr, bias_scr, qz, s_scr, os, att,
    w_sem, wx_ssem, wx_rsem, wo_sem, wox_ssem, wox_rsem,
    kv_ssem, kv_rsem, q_ssem, q_rsem, px_ssem, px_rsem, pl_ssem, pl_rsem, b_ssem, b_rsem,
):
    p = lax.axis_index("peak")
    m = lax.axis_index("mod")
    z = p // 2
    xh = lax.rem(p, 2)
    other = 1 - m

    def step(i):
        near, odd = i // 2, i % 2
        return 4 + (2 * odd - 1) * near + 4 * odd * ((3 - near) // 3)

    def pair_at(i):
        return lax.rem(z + step(i), PAIRS)

    def target(i, dx):
        return 2 * pair_at(i) + lax.rem(xh + dx, 2)

    def source(i, dx):
        return 2 * lax.rem(z + 16 - step(i), PAIRS) + lax.rem(xh + dx, 2)

    def to_peer(src, dst, ssem, rsem, t):
        return pltpu.make_async_remote_copy(
            src, dst, ssem, rsem, device_id={"peak": t}, device_id_type=MESH
        )

    def to_partner(src, dst, ssem, rsem):
        return pltpu.make_async_remote_copy(
            src, dst, ssem, rsem, device_id={"mod": other}, device_id_type=MESH
        )

    def kv_copy(i, dx):
        k = 2 * i + dx
        t = target(i, dx)
        return to_peer(kvs.at[t], kvr.at[k], kv_ssem.at[k], kv_rsem.at[k], t)

    def q_copy(i, dx):
        k = 2 * i + dx
        t = target(i, dx)
        return to_peer(qs.at[t], qr.at[k], q_ssem.at[k], q_rsem.at[k], t)

    def pool_copy(i, dx):
        k = 2 * i + dx
        t = target(i, dx)
        return to_peer(plx.at[t], plr.at[k], pl_ssem.at[k], pl_rsem.at[k], t)

    def back_copy(i, dx):
        k = 2 * i + dx
        return to_peer(os.at[k], att.at[p], b_ssem.at[k], b_rsem.at[k], source(i, dx))

    def pool_swap(i):
        j = pair_at(i)
        return to_partner(
            pls.at[pl.ds(2 * j, 2)], plx.at[pl.ds(2 * j, 2)], px_ssem.at[i], px_rsem.at[i]
        )

    def columns(i):
        j = pair_at(i)
        return w.at[:, pl.ds(pl.multiple_of(j * 384, 128), 384)]

    def w_copy(i):
        return pltpu.make_async_copy(columns(i), w_own.at[i], w_sem.at[i])

    def w_swap(i):
        return to_partner(columns(i), w_oth.at[i], wx_ssem.at[i], wx_rsem.at[i])

    own_rows = pl.ds(pl.multiple_of(m * 512, 512), 512)
    oth_rows = pl.ds(pl.multiple_of(other * 512, 512), 512)
    wo_copy = pltpu.make_async_copy(wo, wo_scr.at[own_rows], wo_sem)
    wo_swap = to_partner(wo, wo_scr.at[own_rows], wox_ssem, wox_rsem)

    barrier = pltpu.get_barrier_semaphore()
    for i in range(PAIRS):
        for dx in range(2):
            if 2 * i + dx != SELF:
                pl.semaphore_signal(
                    barrier, inc=1, device_id={"peak": target(i, dx)}, device_id_type=MESH
                )
    pl.semaphore_signal(barrier, inc=1, device_id={"mod": other}, device_id_type=MESH)

    loads = [
        pltpu.make_async_copy(source_ref, place, in_sem.at[n])
        for n, (source_ref, place) in enumerate((
            (bins_in, bins), (flags_in, flags), (tab_in, tab), (seg_in, seg), (mvec_in, mvec), (hid_in, hid)
        ))
    ]
    for load in loads:
        load.start()
    for i in range(PAIRS):
        w_copy(i).start()
    wo_copy.start()
    for load in loads:
        load.wait()

    tab_scr[...] = jnp.zeros_like(tab_scr)
    tab_scr[0:NBINS] = tab[0]
    row = lax.broadcasted_iota(jnp.int32, (128, TOK), 0)
    onehot = jnp.where(row < 64, (row == bins[...]).astype(F32), (flags[...] == 1).astype(F32))
    picked = onehot.T
    rows_of_bin = dot(picked[:, :64].astype(BF16), tab_scr[...])
    masked = picked[:, 64:65] > 0.5
    chosen = jnp.where(masked, mvec[...].astype(F32), hid[0].astype(F32))
    e_scr[...] = (chosen + rows_of_bin).astype(BF16)

    segment = jnp.bitwise_and(lax.broadcasted_iota(jnp.int32, (16, TOK), 0), 3)
    chosen_seg = (segment == seg[0]).astype(F32)
    counts = jnp.sum(chosen_seg, axis=1, keepdims=True)
    log_counts = jnp.broadcast_to(jnp.log(counts), (16, 128))
    sel = chosen_seg.astype(BF16)
    pool_row = lax.broadcasted_iota(jnp.int32, (16, 128), 0) < 4

    pl.semaphore_wait(barrier, 16)
    for i in range(PAIRS):
        w_swap(i).start()
    wo_swap.start()

    lo = low_lanes(TOK)
    lo_half = low_lanes(HALF)

    def project(i, carry):
        j = pair_at(i)
        w_copy(i).wait()
        w_swap(i).wait_recv()
        pr = dot(e_scr[:, own_rows], w_own[i]) + dot(e_scr[:, oth_rows], w_oth[i])
        t0, t1, t2 = pr[:, 0:128], pr[:, 128:256], pr[:, 256:384]
        r0 = pltpu.roll(t0, 64, 1)
        r1 = pltpu.roll(t1, 64, 1)
        kv0 = jnp.where(lo, r0, r1).astype(BF16)
        kv1 = t2.astype(BF16)
        kvs[2 * j] = kv0
        kvs[2 * j + 1] = kv1
        for dx in range(2):
            @pl.when(2 * i + dx != SELF)
            def _():
                kv_copy(i, dx).start()
        q0 = jnp.where(lo_half, t0[:HALF], r0[HALF:])
        q1 = jnp.where(lo_half, r1[:HALF], t1[HALF:])
        qs[2 * j] = (q0 * 0.125).astype(BF16)
        qs[2 * j + 1] = (q1 * 0.125).astype(BF16)
        pls[2 * j] = jnp.where(pool_row, dot(sel, kv0) / counts, log_counts).astype(BF16)
        pls[2 * j + 1] = jnp.where(pool_row, dot(sel, kv1) / counts, log_counts).astype(BF16)
        pool_swap(i).start()
        return carry

    lax.fori_loop(0, PAIRS, project, 0)
    kvr[SELF] = kvs[p]
    qr[SELF] = qs[p]

    def forward(i, carry):
        pool_swap(i).wait_recv()
        for dx in range(2):
            @pl.when(2 * i + dx != SELF)
            def _():
                pool_copy(i, dx).start()
        return carry

    lax.fori_loop(0, PAIRS, forward, 0)
    plr[SELF] = plx[p]

    def sent_kv(i, carry):
        for dx in range(2):
            @pl.when(2 * i + dx != SELF)
            def _():
                kv_copy(i, dx).wait_send()
        return carry

    lax.fori_loop(0, PAIRS, sent_kv, 0)

    def each_in(g, action):
        for kk in range(GROUP):
            i = g * (GROUP // 2) + kk // 2
            dx = kk % 2

            @pl.when(2 * i + dx != SELF)
            def _():
                action(i, dx)

    each_in(0, lambda i, dx: q_copy(i, dx).start())
    each_in(1, lambda i, dx: q_copy(i, dx).start())

    def take_values(i, carry):
        for dx in range(2):
            @pl.when(2 * i + dx != SELF)
            def _():
                kv_copy(i, dx).wait_recv()
        block = kvr[pl.ds(2 * i, 2)].reshape(2 * TOK, 128).astype(F32).T
        vt[:, pl.ds(pl.multiple_of(i * 384, 128), 384)] = block[64:128].astype(BF16)
        return carry

    lax.fori_loop(0, PAIRS, take_values, 0)

    def take_pooled(i, carry):
        for dx in range(2):
            @pl.when(2 * i + dx != SELF)
            def _():
                pool_copy(i, dx).wait_recv()
        return carry

    lax.fori_loop(0, PAIRS, take_pooled, 0)
    pooled = plr[...].reshape(NP * 16, 128)
    summary = lax.broadcasted_iota(jnp.int32, (64, 256), 0)
    place = (summary // 4) * 16 + jnp.bitwise_and(summary, 3)
    column = lax.broadcasted_iota(jnp.int32, (64, 256), 1)
    pk = dot((column == place).astype(BF16), pooled)
    pk_scr[...] = pk.astype(BF16)
    bias_scr[...] = dot((column == place + 4).astype(BF16), pooled)
    pk_pad = jnp.concatenate([pk, jnp.zeros((64, 128), F32)], axis=0).T
    pvt_scr[...] = pk_pad[64:128].astype(BF16)

    cols = GROUP * TOK
    n_chunks = NP * TOK // CHUNK

    def attend(g, carry):
        each_in(g, lambda i, dx: q_copy(i, dx).wait_recv())

        @pl.when(g == 0)
        def _():
            each_in(2, lambda i, dx: q_copy(i, dx).start())
            each_in(3, lambda i, dx: q_copy(i, dx).start())
        for kk in range(GROUP):
            i = g * (GROUP // 2) + kk // 2
            dx = kk % 2

            a = qr[2 * i + dx].astype(F32)
            top = jnp.where(lo_half, a, 0.0)
            bottom = jnp.where(lo_half, pltpu.roll(a, 64, 1), 0.0)
            qz[kk * TOK:kk * TOK + HALF] = top.astype(BF16)
            qz[kk * TOK + HALF:(kk + 1) * TOK] = bottom.astype(BF16)
        s_pool = dot_t(pk_scr[...], qz[...]) + bias_scr[:, 0:1]
        m8 = jnp.max(s_pool.reshape(8, 8, cols), axis=0)

        def score(c, m8):
            keys = kvr[pl.ds(c * (CHUNK // TOK), CHUNK // TOK)].reshape(CHUNK, 128)
            s = dot_t(keys, qz[...])
            s_scr[pl.ds(pl.multiple_of(c * CHUNK, CHUNK), CHUNK)] = s
            return jnp.maximum(m8, jnp.max(s.reshape(CHUNK // 8, 8, cols), axis=0))

        m8 = lax.fori_loop(0, n_chunks, score, m8)
        top_score = jnp.max(m8, axis=0, keepdims=True)
        w_pool = jnp.exp(s_pool - top_score)
        l8 = jnp.sum(w_pool.reshape(8, 8, cols), axis=0)
        acc_o = dot(pvt_scr[:, 0:64], w_pool.astype(BF16))

        def weigh(c, state):
            l8, acc_o = state
            s = s_scr[pl.ds(pl.multiple_of(c * CHUNK, CHUNK), CHUNK)]
            wt = jnp.exp(s - top_score)
            l8 = l8 + jnp.sum(wt.reshape(CHUNK // 8, 8, cols), axis=0)
            values = vt[:, pl.ds(pl.multiple_of(c * CHUNK, 128), CHUNK)]
            return l8, acc_o + dot(values, wt.astype(BF16))

        l8, acc_o = lax.fori_loop(0, n_chunks, weigh, (l8, acc_o))
        attended = (acc_o / jnp.sum(l8, axis=0, keepdims=True)).T
        for kk in range(GROUP):
            i = g * (GROUP // 2) + kk // 2
            dx = kk % 2
            rows = attended[kk * TOK:(kk + 1) * TOK]
            packed = jnp.concatenate([rows[:HALF], rows[HALF:]], axis=1).astype(BF16)
            os[2 * i + dx] = packed

            @pl.when(2 * i + dx != SELF)
            def _():
                back_copy(i, dx).start()

            @pl.when(2 * i + dx == SELF)
            def _():
                att[p] = packed
        return carry

    lax.fori_loop(0, NP // GROUP, attend, 0)


    def take_back(i, carry):
        for dx in range(2):
            @pl.when(2 * i + dx != SELF)
            def _():
                back_copy(i, dx).wait_recv()
        return carry

    lax.fori_loop(0, PAIRS, take_back, 0)
    for j in range(PAIRS):
        a = att[2 * j].astype(F32)
        b = att[2 * j + 1].astype(F32)
        top = jnp.where(lo_half, a, pltpu.roll(b, 64, 1))
        bottom = jnp.where(lo_half, pltpu.roll(a, 64, 1), b)
        e_scr[0:HALF, j * 128:(j + 1) * 128] = top.astype(BF16)
        e_scr[HALF:TOK, j * 128:(j + 1) * 128] = bottom.astype(BF16)
    wo_copy.wait()
    wo_swap.wait_recv()
    out[0] = dot(e_scr[...], wo_scr[...]).astype(BF16)

    def drain(i, carry):
        for dx in range(2):
            @pl.when(2 * i + dx != SELF)
            def _():
                q_copy(i, dx).wait_send()
                pool_copy(i, dx).wait_send()
                back_copy(i, dx).wait_send()
        pool_swap(i).wait_send()
        w_swap(i).wait_send()
        return carry

    lax.fori_loop(0, PAIRS, drain, 0)
    wo_swap.wait_send()


def shards(hidden_in, value_bins, mask_flags, segment_ids, bin_table, mask_vector, qkv_weight, out_weight):
    vmem = pl.BlockSpec(memory_space=pltpu.VMEM)
    hbm = pl.BlockSpec(memory_space=pltpu.MemorySpace.HBM)
    dma = pltpu.SemaphoreType.DMA
    return pl.pallas_call(
        kernel,
        out_shape=jax.ShapeDtypeStruct((1, TOK, WIDTH), BF16),
        in_specs=[hbm] * 8,
        out_specs=vmem,
        scratch_shapes=[
            pltpu.VMEM(hidden_in.shape, BF16),
            pltpu.VMEM(value_bins.shape, jnp.int32),
            pltpu.VMEM(mask_flags.shape, jnp.int32),
            pltpu.VMEM(segment_ids.shape, jnp.int32),
            pltpu.VMEM(bin_table.shape, BF16),
            pltpu.VMEM(mask_vector.shape, BF16),
            dma((6,)),
            pltpu.VMEM((TOK, WIDTH), BF16),
            pltpu.VMEM((64, WIDTH), BF16),
            pltpu.VMEM((PAIRS, 512, 384), BF16),
            pltpu.VMEM((PAIRS, 512, 384), BF16),
            pltpu.VMEM((WIDTH, WIDTH), BF16),
            pltpu.VMEM((NP, TOK, 128), BF16),
            pltpu.VMEM((NP, TOK, 128), BF16),
            pltpu.VMEM((NP, HALF, 128), BF16),
            pltpu.VMEM((NP, HALF, 128), BF16),
            pltpu.VMEM((NP, 16, 128), BF16),
            pltpu.VMEM((NP, 16, 128), BF16),
            pltpu.VMEM((NP, 16, 128), BF16),
            pltpu.VMEM((64, NP * TOK), BF16),
            pltpu.VMEM((64, 128), BF16),
            pltpu.VMEM((64, 128), BF16),
            pltpu.VMEM((64, 128), F32),
            pltpu.VMEM((GROUP * TOK, 128), BF16),
            pltpu.VMEM((NP * TOK, GROUP * TOK), F32),
            pltpu.VMEM((NP, HALF, 128), BF16),
            pltpu.VMEM((NP, HALF, 128), BF16),
            dma((PAIRS,)), dma((PAIRS,)), dma((PAIRS,)),
            dma, dma, dma,
            dma((NP,)), dma((NP,)), dma((NP,)), dma((NP,)),
            dma((PAIRS,)), dma((PAIRS,)), dma((NP,)), dma((NP,)), dma((NP,)), dma((NP,)),
        ],
        compiler_params=pltpu.CompilerParams(
            collective_id=0, has_side_effects=True, vmem_limit_bytes=48 << 20
        ),
        cost_estimate=pl.CostEstimate(
            flops=4 * 10**9, bytes_accessed=10 * 2**20, transcendentals=10**7
        ),
    )(*[
        pltpu.with_memory_space_constraint(x, pltpu.MemorySpace.HBM)
        for x in (
            hidden_in, value_bins, mask_flags, segment_ids,
            bin_table, mask_vector, qkv_weight, out_weight,
        )
    ])


def solution(mesh):
    placed = (
        P("mod", ("dp", "peak"), None),
        P("mod", ("dp", "peak")),
        P("mod", ("dp", "peak")),
        P("mod", ("dp", "peak"), None),
        P("mod", None, None),
        P("mod", None),
        P("mod", None),
        P("mod", None),
    )
    return jax.shard_map(
        shards,
        mesh=mesh,
        in_specs=placed,
        out_specs=P("mod", ("dp", "peak"), None),
        check_vma=False,
    )
```
